32 devices in a mesh: grp: 4 (over x, core), tbl: 8 (over z, y).
Axes of the slice: x: 2, y: 2, z: 4, core: 2. Of those that a mesh axis runs over, the one named last changes fastest.
Arguments:
- cross_input: bfloat16 [4096, 3456], P(('grp', 'tbl')), may hold values from -6 to 6
- upstream: bfloat16 [4096, 3456], P(('grp', 'tbl')), may hold values from -6 to 6
- v_weight: bfloat16 [256, 3456], replicated, may hold values from -0.109375 to 0.109375
- u_weight: bfloat16 [256, 3456], replicated, may hold values from -0.375 to 0.375
- bias: float32 [3456], replicated, may hold values from -3 to 3
- placement: int32 [26], replicated, may hold values from 0 to 7, as said below
- owned_ids: int32 [40, 4, 4096], P('tbl', None, 'grp'), may hold values from 0 to 255
Outputs:
- cross_grad: float32 [256, 6912], P(('grp', 'tbl'))
- table_grad: float32 [40, 256, 128], P('tbl', 'grp')
The draws below stay inside these ranges and needn't reach their ends.
Inputs may be any that keep to these rules, and one draw needn't show every extreme that they name: `placement`: no device holds more than 5 tables, and some device holds exactly 5.
All inputs are finite; a program needn't handle non-finite values.
Results may differ from the reference program's by a relative error of at most 0.004.
Values may be sent and summed in bfloat16 or wider, within the bound.
A program may use at most 64 MiB of HBM per device.

```python
import math
import jax
import jax.numpy as jnp
import numpy as np
from jax import lax

EMB = 128
TABLES = 26
D = 3456
RANK = 256
TOK_DEV = 128
HOT = 4
ROWS = 256
MAXT = 5
SLOTS = 40
TOKENS = 4096
N_TBL = 8
DEVICES = 32


def draw_placement(key, part):
    key_heavy = jax.random.fold_in(key, 11)
    key_score = jax.random.fold_in(key, 12)
    key_order = jax.random.fold_in(key, 13)
    total = N_TBL * MAXT
    heavy = jax.random.randint(key_heavy, (), 0, N_TBL)
    score = jax.random.permutation(key_score, total).astype(jnp.int32)
    slot_ids = jnp.arange(total, dtype=jnp.int32)
    score = jnp.where(slot_ids // MAXT == heavy, total + slot_ids, score)
    unused, chosen = lax.top_k(score, TABLES)
    order = jax.random.permutation(key_order, TABLES)
    return (chosen // MAXT)[order].astype(jnp.int32)


def place_ends(result, own_key, low, high):
    dims = result.shape
    place = [jax.random.randint(jax.random.fold_in(own_key, axis), (), 0, dims[axis]) for axis in range(len(dims))]
    result = result.at[tuple(place)].set(low)
    longest = dims.index(max(dims))
    place[longest] = (place[longest] + 1) % dims[longest]
    return result.at[tuple(place)].set(high)


def level_of(rng, dims, pieces, smallest, top_value):
    level, own = 1.0, jax.random.fold_in(rng, 6)
    for dim, blocks in pieces:
        steps = jnp.exp(jax.random.uniform(jax.random.fold_in(own, dim), (blocks,), jnp.float32, smallest / len(pieces), top_value / len(pieces)))
        level = level * jnp.repeat(steps, dims[dim] // blocks).reshape([-1 if axis == dim else 1 for axis in range(len(dims))])
    return level


def rank_bounds(count, slope):
    portions = [(1 << 20) // math.isqrt(standing ** slope) + 1 for standing in range(1, count + 1)]
    spread = 1 + sum(portions) // (1 << 30)
    return np.cumsum(np.array([max(1, weight // spread) for weight in portions]))


def skewed_ids(rng, shape, number_of, slope):
    grid = rank_bounds(number_of, slope)
    pick = jax.random.randint(jax.random.fold_in(rng, 1), shape, 0, int(grid[number_of - 1]))
    standing = jnp.searchsorted(jnp.asarray(grid, jnp.int32), pick, side="right")
    return jax.random.permutation(jax.random.fold_in(rng, 2), number_of)[standing].astype(jnp.int32)


def centred(rng, shape, scale, bound, pieces=(), held_as=jnp.bfloat16):
    drawn = jax.random.normal(rng, shape, jnp.float32) * scale
    if len(pieces) > 0:
        drawn = level_of(rng, shape, pieces, -0.22, 0.18) * drawn
    return jnp.clip(drawn, min=-bound, max=bound).astype(held_as)


def setup_inputs(seed: int = 0) -> dict:
    streams_of = jax.random.split(jax.random.key(seed), 8)
    return {
        "cross_input": centred(streams_of[0], (TOKENS, D), 1.0, 6.0, ((0, 32),)),
        "upstream": centred(streams_of[1], (TOKENS, D), 1.0, 6.0, ((0, 32),)),
        "v_weight": centred(streams_of[2], (RANK, D), D ** -0.5, 0.109375),
        "u_weight": centred(streams_of[3], (RANK, D), RANK ** -0.5, 0.375),
        "bias": centred(streams_of[4], (D,), 0.5, 3.0, (), jnp.float32),
        "placement": draw_placement(jax.random.fold_in(streams_of[7], 71), 0),
        "owned_ids": place_ends(skewed_ids(streams_of[6], (SLOTS, HOT, TOKENS), ROWS, 1), jax.random.fold_in(streams_of[6], 3), 0, ROWS - 1).astype(jnp.int32),
    }


def block_terms(cross_input, upstream, v_weight, u_weight, bias):
    hidden = jnp.dot(cross_input, v_weight.T, preferred_element_type=jnp.float32).astype(jnp.bfloat16)
    mixed = jnp.dot(hidden, u_weight, preferred_element_type=jnp.float32) + bias
    up_float = upstream.astype(jnp.float32)
    product_grad = (up_float * cross_input.astype(jnp.float32)).astype(jnp.bfloat16)
    grad_u = jnp.dot(hidden.T, product_grad, preferred_element_type=jnp.float32)
    hidden_grad = jnp.dot(product_grad, u_weight.T, preferred_element_type=jnp.float32).astype(jnp.bfloat16)
    grad_v = jnp.dot(hidden_grad.T, cross_input, preferred_element_type=jnp.float32)
    input_grad = up_float * (1.0 + mixed) + jnp.dot(hidden_grad, v_weight, preferred_element_type=jnp.float32)
    pooled = input_grad[:, EMB:].astype(jnp.bfloat16)
    return (grad_u, grad_v, pooled)

def reference(cross_input, upstream, v_weight, u_weight, bias, placement, owned_ids):
    inputs_blocks = cross_input.reshape(DEVICES, TOK_DEV, D)
    upstream_blocks = upstream.reshape(DEVICES, TOK_DEV, D)

    def advance(carry, item):
        grad_u, grad_v, pooled = block_terms(item[0], item[1], v_weight, u_weight, bias)
        return ((carry[0] + grad_u, carry[1] + grad_v), pooled)
    start = (jnp.zeros((RANK, D), jnp.float32), jnp.zeros((RANK, D), jnp.float32))
    sums, pooled = lax.scan(advance, start, (inputs_blocks, upstream_blocks))
    cross_grad = jnp.concatenate([sums[0], sums[1]], axis=1) * (1.0 / math.sqrt(TOKENS))
    pooled = pooled.reshape(TOKENS, TABLES, EMB)
    same = placement[:, None] == placement[None, :]
    earlier = jnp.arange(TABLES)[None, :] < jnp.arange(TABLES)[:, None]
    slot = lax.optimization_barrier(jnp.sum((same & earlier).astype(jnp.int32), axis=1)).astype(jnp.int32)
    target = (placement * MAXT + slot).astype(jnp.int32)
    table_grad = jnp.zeros((SLOTS, ROWS, EMB), jnp.float32)
    for table in range(TABLES):
        values = pooled[:, table, :].astype(jnp.float32)
        row_ids = owned_ids[target[table]]
        total = jnp.zeros((ROWS, EMB), jnp.float32)
        for lookup in range(HOT):
            total = total + jax.ops.segment_sum(values, row_ids[lookup], num_segments=ROWS)
        table_grad = table_grad.at[target[table]].add(total)
    return (cross_grad, table_grad)
```

```python
import functools
import math

import jax
import jax.numpy as jnp
from jax import lax
from jax.experimental import pallas as pl
from jax.experimental.pallas import tpu as pltpu
from jax.sharding import PartitionSpec as P

EMB = 128
TABLES = 26
ROWS = 256
MESH = pl.DeviceIdType.MESH


def outer_sum(left, right):
    return jnp.einsum("br,bd->rd", left, right, preferred_element_type=jnp.float32)


def on_device(cross_input, upstream, v_weight, u_weight, bias, placement, owned_ids):
    n_grp = lax.axis_size("grp")
    n_tbl = lax.axis_size("tbl")
    samples = cross_input.shape[0]
    slots_dev = owned_ids.shape[0]
    scale = 1.0 / math.sqrt(samples * n_grp * n_tbl)
    hidden = jnp.dot(cross_input, v_weight.T, preferred_element_type=jnp.float32).astype(
        jnp.bfloat16
    )
    mixed = jnp.dot(hidden, u_weight, preferred_element_type=jnp.float32) + bias
    up_float = upstream.astype(jnp.float32)
    product_grad = (up_float * cross_input.astype(jnp.float32)).astype(jnp.bfloat16)
    hidden_grad = jnp.dot(product_grad, u_weight.T, preferred_element_type=jnp.float32).astype(
        jnp.bfloat16
    )
    input_grad = up_float * (1.0 + mixed) + jnp.dot(
        hidden_grad, v_weight, preferred_element_type=jnp.float32
    )
    pooled = input_grad[:, EMB:].astype(jnp.bfloat16).reshape(samples, TABLES, EMB)
    same = placement[:, None] == placement[None, :]
    earlier = jnp.arange(TABLES)[None, :] < jnp.arange(TABLES)[:, None]
    slot = jnp.sum((same & earlier).astype(jnp.int32), axis=1)
    target = slot * n_tbl + placement
    select = (jnp.arange(slots_dev * n_tbl, dtype=jnp.int32)[:, None] == target[None, :]).astype(
        jnp.bfloat16
    )
    outgoing = jnp.einsum("st,bte->sbe", select, pooled, preferred_element_type=jnp.float32)
    outgoing = outgoing.astype(jnp.bfloat16).reshape(slots_dev, n_tbl, samples, EMB)
    arriving = lax.all_to_all(outgoing, "tbl", split_axis=1, concat_axis=1, tiled=True)
    arriving = arriving.reshape(slots_dev, n_tbl * samples, EMB)
    row_numbers = jnp.arange(ROWS, dtype=jnp.int32)
    counts = jnp.sum(
        (owned_ids[:, :, None, :] == row_numbers[None, None, :, None]).astype(jnp.bfloat16), axis=1
    )
    row_terms = jnp.einsum("srm,sme->sre", counts, arriving, preferred_element_type=jnp.float32)
    table_grad = lax.psum_scatter(row_terms, "grp", scatter_dimension=1, tiled=True)
    term = jnp.concatenate(
        [outer_sum(hidden, product_grad), outer_sum(hidden_grad, cross_input)], axis=1
    )
    summed = lax.psum_scatter(term, ("grp", "tbl"), scatter_dimension=0, tiled=True)
    cross_grad = summed * scale
    return (cross_grad, table_grad)


def halving_fits(n_grp, n_tbl):
    return n_grp == 4 and n_tbl == 8


CANON = "xhly"


def left_over(done):
    return [d for d in CANON if d not in done]


def lead_of(done):
    return (2,) * len(left_over(done))


def plan_of(width):
    tiles = width // EMB
    ends = [tiles * n // 27 * EMB for n in (0, 6, 9, 13, 16, 20, 24, 27)]
    dims = ("yxlh", "lhyx", "yxlh", "lhyx", "lhxy", "ylxh", "ylxh")
    cross = {}
    for i, name in enumerate("abcdefg"):
        cross[name] = (("u", ends[i]), ("v", ends[i]), ends[i + 1] - ends[i], dims[i])
    table = {}
    for i, rest in enumerate(("yhl", "ylh", "ylh", "lyh")):
        table["ABCD"[i]] = (i, i + 1, "x" + rest)
    groups = (0, 8, 16, 22, 26)
    order = (
        ["Xb", "Xg", "T0", "Xa", "Xd", "T1", "Xf", "Xe", "Xc", "T2", "T3", "b1", "g1", "d1", "a1", "e1", "b2", "g2", "f1", "A1", "B1", "C1", "D1", "d2", "c1", "a2", "b3", "g3", "f2", "e2", "A2", "c2", "D2", "b4", "B2", "e3", "a3", "f3", "g4", "C2", "d3", "c3", "A3", "D3", "B3", "e4", "d4", "a4", "f4", "C3", "A4", "c4", "B4", "D4", "C4"]
    )
    return cross, table, groups, order


def scratch_of(samples, width, rank, n_tbl, slots_dev, hot, part, plan):
    f32, bf16, i32 = jnp.float32, jnp.bfloat16, jnp.int32
    V = pltpu.VMEM
    cross, table, groups, order = plan
    rows = part // len(table)
    out = {
        "ci": V((2 * samples, width), bf16),
        "up": V((2 * samples, width), bf16),
        "v": V((rank, width), bf16),
        "u": V((rank, width), bf16),
        "pg": V((2 * samples, width), bf16),
        "hid": V((2 * samples, rank), bf16),
        "hgr": V((2 * samples, rank), bf16),
        "hid_t": V((2, rank, samples), bf16),
        "hgr_t": V((2, rank, samples), bf16),
        "ids": V((2, n_tbl, slots_dev, hot, samples), i32),
        "slot": pltpu.SMEM((TABLES,), i32),
        "inv": pltpu.SMEM((slots_dev * n_tbl,), i32),
        "load_sem": pltpu.SemaphoreType.DMA((4,)),
        "in_s": pltpu.SemaphoreType.DMA((10,)),
        "in_r": pltpu.SemaphoreType.DMA((10,)),
        "id_s": pltpu.SemaphoreType.DMA((2, n_tbl)),
        "id_r": pltpu.SemaphoreType.DMA((2, n_tbl)),
        "ssem": pltpu.SemaphoreType.DMA((64,)),
        "rsem": pltpu.SemaphoreType.DMA((64,)),
        "st": V((TABLES, part, EMB), bf16),
        "rt": V((TABLES, part, EMB), bf16),
        "ot": V((TABLES, part, EMB), f32),
    }
    for name, (top, bottom, wide, dims) in cross.items():
        for k in range(4):
            shape = lead_of(dims[: k + 1]) + (16, wide)
            out["s%s%d" % (name, k)] = V(shape, bf16)
            out["r%s%d" % (name, k)] = V(shape, bf16)
            out["o%s%d" % (name, k)] = V(shape, f32)
    for name, (lo, hi, dims) in table.items():
        for k in range(1, 4):
            shape = lead_of(dims[: k + 1]) + (slots_dev, rows, EMB)
            out["s%s%d" % (name, k)] = V(shape, bf16)
            out["r%s%d" % (name, k)] = V(shape, bf16)
            out["o%s%d" % (name, k)] = V(shape, f32)
    return out


def fused_body(n_grp, n_tbl, scale, plan, names, *refs):
    f32, bf16 = jnp.float32, jnp.bfloat16
    ci_hbm, up_hbm, v_hbm, u_hbm, bias_ref, place_ref, ids_hbm, cross_ref, table_ref = refs[:9]
    r = dict(zip(names, refs[9:]))
    cross, table, groups, order = plan
    g = lax.axis_index("grp")
    t = lax.axis_index("tbl")
    core, x = g % 2, g // 2
    y, zl, zh = t % 2, (t // 2) % 2, t // 4
    og = g + 1 - 2 * core
    bits = {"x": x, "h": zh, "l": zl, "y": y}
    peers = {
        "x": (core + 2 * (1 - x), t),
        "y": (g, t + 1 - 2 * y),
        "l": (g, t + 2 * (1 - 2 * zl)),
        "h": (g, t + 4 * (1 - 2 * zh)),
    }
    samples, width = ci_hbm.shape
    rank = v_hbm.shape[0]
    slots_dev = ids_hbm.shape[0]
    part = ROWS // n_grp
    rows = part // len(table)
    quarter = rank // n_grp

    barrier = pltpu.get_barrier_semaphore()

    def greet(gg, tt):
        pl.semaphore_signal(barrier, inc=1, device_id=(gg, tt), device_id_type=MESH)

    for step in range(1, n_tbl):
        greet(g, (t + step) % n_tbl)
        greet(og, (t + step) % n_tbl)
    greet(og, t)
    greet(*peers["x"])

    own_rows, their_rows = pl.ds(0, samples), pl.ds(samples, samples)
    loads = [
        pltpu.make_async_copy(src, dst, r["load_sem"].at[i])
        for i, (src, dst) in enumerate(
            (
                (ci_hbm, r["ci"].at[own_rows]),
                (v_hbm, r["v"]),
                (up_hbm, r["up"].at[own_rows]),
                (u_hbm, r["u"]),
            )
        )
    ]
    for load in loads:
        load.start()

    pl.semaphore_wait(barrier, 2 * n_tbl)

    def remote(src, dst, s, rs, peer):
        copy = pltpu.make_async_remote_copy(
            src_ref=src, dst_ref=dst, send_sem=s, recv_sem=rs,
            device_id=peer, device_id_type=MESH,
        )
        copy.start()
        return copy

    sems = iter(range(64))

    def send(src, dst, peer):
        i = next(sems)
        return remote(src, dst, r["ssem"].at[i], r["rsem"].at[i], peer)

    thirds = [width // EMB * i // 3 * EMB for i in range(4)]
    moves = []
    for i in range(3):
        cols = pl.ds(thirds[i], thirds[i + 1] - thirds[i])
        moves.append((ci_hbm.at[:, cols], r["ci"].at[their_rows, cols]))
        moves.append((up_hbm.at[:, cols], r["up"].at[their_rows, cols]))
    raw = [
        remote(src, dst, r["in_s"].at[i], r["in_r"].at[i], (og, t))
        for i, (src, dst) in enumerate(moves)
    ]
    id_copies = []
    for step in range(n_tbl):
        to = (t + step) % n_tbl
        block = ids_hbm.at[:, :, pl.ds(pl.multiple_of(to * samples, samples), samples)]
        if step == 0:
            mine = pltpu.make_async_copy(block, r["ids"].at[0, t], r["id_s"].at[0, 0])
            mine.start()
        else:
            id_copies.append(
                remote(
                    block, r["ids"].at[0, t], r["id_s"].at[0, step], r["id_r"].at[0, step], (g, to)
                )
            )
        id_copies.append(
            remote(block, r["ids"].at[1, t], r["id_s"].at[1, step], r["id_r"].at[1, step], (og, to))
        )

    nt = (((1,), (1,)), ((), ()))

    def by_position(value):
        blocks = []
        for gg in range(n_grp):
            for pos in range(n_tbl):
                yy, ll, hh = pos // 4, (pos // 2) % 2, pos % 2
                at = gg * quarter + 8 * (hh * 4 + ll * 2 + yy)
                blocks.append(value[at : at + 8])
        return jnp.concatenate(blocks, axis=0).astype(bf16)

    loads[0].wait()
    loads[1].wait()
    hidden = lax.dot_general(r["ci"][own_rows, :], r["v"][...], nt, preferred_element_type=f32)
    r["hid"][own_rows, :] = hidden.astype(bf16)
    r["hid_t"][0] = by_position(hidden.T)
    at = 6
    ready = []
    for i, (src, dst) in enumerate(
        (
            (r["hid_t"].at[0], r["hid_t"].at[1]),
            (r["hid"].at[own_rows], r["hid"].at[their_rows]),
        )
    ):
        ready.append(remote(src, dst, r["in_s"].at[at + i], r["in_r"].at[at + i], (og, t)))
    loads[2].wait()
    loads[3].wait()
    places = [place_ref[i] for i in range(TABLES)]
    targets = []
    for i in range(TABLES):
        slot = jnp.int32(0)
        for j in range(i):
            slot += (places[j] == places[i]).astype(jnp.int32)
        r["slot"][i] = jnp.minimum(slot, slots_dev - 1)
        targets.append(places[i] * slots_dev + slot)
    for q in range(slots_dev * n_tbl):
        which = jnp.int32(-1)
        for i in range(TABLES):
            which = jnp.where(targets[i] == q, i, which)
        r["inv"][q] = which
    r["pg"][own_rows, :] = (
        r["up"][own_rows, :].astype(f32) * r["ci"][own_rows, :].astype(f32)
    ).astype(bf16)
    hgrad = lax.dot_general(r["pg"][own_rows, :], r["u"][...], nt, preferred_element_type=f32)
    r["hgr"][own_rows, :] = hgrad.astype(bf16)
    r["hgr_t"][0] = by_position(hgrad.T)
    for i, (src, dst) in enumerate(
        (
            (r["hgr_t"].at[0], r["hgr_t"].at[1]),
            (r["hgr"].at[own_rows], r["hgr"].at[their_rows]),
        )
    ):
        ready.append(remote(src, dst, r["in_s"].at[at + 2 + i], r["in_r"].at[at + 2 + i], (og, t)))

    index = lax.broadcasted_iota(jnp.int32, (2 * part, 2 * samples), 0)
    side_of = jnp.where(index // part == 0, x, 1 - x)
    row_of = ((side_of * 2 + core) * part + index % part).astype(f32).astype(bf16)

    def tables(pair):
        cols = pl.ds(EMB + pair * 2 * EMB, 2 * EMB)
        shift = jnp.concatenate(
            [bias_ref[pl.ds(1 + 2 * pair, 1), :], bias_ref[pl.ds(2 + 2 * pair, 1), :]], axis=1
        )
        mixed = jnp.dot(r["hid"][...], r["u"][:, cols], preferred_element_type=f32) + shift
        back = jnp.dot(r["hgr"][...], r["v"][:, cols], preferred_element_type=f32)
        pooled = (r["up"][:, cols].astype(f32) * (1.0 + mixed) + back).astype(bf16)
        for piece in range(2):
            which = pair * 2 + piece
            owner, slot = place_ref[which], r["slot"][which]
            looked = jnp.concatenate([r["ids"][0, owner, slot], r["ids"][1, owner, slot]], axis=1)
            looked = looked.astype(f32).astype(bf16)
            one, zero = jnp.bfloat16(1), jnp.bfloat16(0)
            count = jnp.zeros((2 * part, 2 * samples), bf16)
            for k in range(looked.shape[0]):
                count += jnp.where(looked[k : k + 1, :] == row_of, one, zero)
            sums = jnp.dot(
                count, pooled[:, piece * EMB : (piece + 1) * EMB], preferred_element_type=f32
            )
            r["ot"][which] = sums[:part]
            r["st"][which] = sums[part:].astype(bf16)

    def picked(ref, first):
        def take(gg, start, size):
            at = pl.ds(pl.multiple_of(gg * quarter + start, size), size)
            return jnp.concatenate([ref[0, at, :], ref[1, at, :]], axis=1)

        out = []
        for side in range(2):
            bit = bits[first] if side == 0 else 1 - bits[first]
            if first == "x":
                out.append(take(core + 2 * bit, 0, quarter))
                continue
            for xx in range(2):
                if first == "y":
                    out.append(take(core + 2 * xx, bit * (quarter // 2), quarter // 2))
                else:
                    for yy in range(2):
                        out.append(
                            take(
                                core + 2 * xx, yy * (quarter // 2) + bit * (quarter // 4), quarter // 4
                            )
                        )
        return jnp.concatenate(out, axis=0)

    def place_of(first, i):
        a, b, c = i // 4, (i // 2) % 2, i % 2
        if first == "y":
            return (a, c, b)
        if first == "l":
            return (a, c, b)
        return (c, b, a)

    flying, chosen, waited = {}, {}, set()

    def await_all(key, copies):
        if key not in waited:
            waited.add(key)
            for copy in copies:
                copy.wait()

    def raw_ready(lo, hi):
        for i in range(3):
            if lo < thirds[i + 1] and hi > thirds[i]:
                await_all("raw%d" % i, raw[2 * i : 2 * i + 2])

    made_pg = set()

    def factors(kind, first):
        index = 0 if kind == "u" else 2
        await_all("ready%d" % index, [ready[index]])
        if (kind, first) not in chosen:
            chosen[kind, first] = picked(r["hid_t" if kind == "u" else "hgr_t"], first)
        return chosen[kind, first]

    def product(kind, lhs, lo, hi):
        if kind == "v":
            return jnp.dot(lhs, r["ci"][:, lo:hi], preferred_element_type=f32)
        theirs = (
            r["up"][their_rows, lo:hi].astype(f32) * r["ci"][their_rows, lo:hi].astype(f32)
        ).astype(bf16)
        both = jnp.concatenate([r["pg"][own_rows, lo:hi], theirs], axis=0)
        return jnp.dot(lhs, both, preferred_element_type=f32)

    def cross_piece(name):
        top, bottom, wide, dims = cross[name]
        for kind, lo in (top, bottom):
            raw_ready(lo, lo + wide)
        for off in range(0, wide, 512):
            end = min(off + 512, wide)
            halves = []
            for kind, lo in (top, bottom):
                halves.append(product(kind, factors(kind, dims[0]), lo + off, lo + end))
            for i in range(2 * n_tbl):
                tile = jnp.concatenate([h[8 * i : 8 * i + 8] for h in halves], axis=0)
                at = place_of(dims[0], i % n_tbl) + (slice(None), slice(off, end))
                if i < n_tbl:
                    r["o%s0" % name][at] = tile
                else:
                    r["s%s0" % name][at] = tile.astype(bf16)
        flying[name] = send(r["s%s0" % name], r["r%s0" % name], peers[dims[0]])

    def table_group(n):
        await_all("ready1", [ready[1]])
        await_all("ready3", [ready[3]])
        raw_ready(EMB * (1 + groups[n]), EMB * (1 + groups[n + 1]))
        await_all("ids", [mine] + id_copies)
        for pair in range(groups[n] // 2, groups[n + 1] // 2):
            tables(pair)
        at = pl.ds(groups[n], groups[n + 1] - groups[n])
        flying["T%d" % n] = send(r["st"].at[at], r["rt"].at[at], peers["x"])

    def indices(depth):
        out = [()]
        for _ in range(depth):
            out = [i + (j,) for i in out for j in range(2)]
        return out

    def halve(name, dims, k):
        flying[name].wait()
        own, came = r["o%s%d" % (name, k)], r["r%s%d" % (name, k)]
        kept, out = r["o%s%d" % (name, k + 1)], r["s%s%d" % (name, k + 1)]
        axis = left_over(dims[: k + 1]).index(dims[k + 1])
        bit = bits[dims[k + 1]]

        def fill(dst, b, kind):
            for i in indices(2 - k):
                at = i[:axis] + (b,) + i[axis:]
                value = (own[at] + came[at].astype(f32)).astype(kind)
                if i:
                    dst[i] = value
                else:
                    dst[...] = value

        fill(out, 1 - bit, bf16)
        flying[name] = send(out, r["r%s%d" % (name, k + 1)], peers[dims[k + 1]])
        fill(kept, bit, f32)

    def spread(name):
        lo, hi, dims = table[name]
        for n in range(len(groups) - 1):
            await_all("T%d" % n, [flying["T%d" % n]])
        others = left_over(dims[:2])
        weight = {"h": 4, "l": 2, "y": 1}
        at_rows = pl.ds(lo * rows, (hi - lo) * rows)

        def each_slot(bit, dst, kind):
            def run(i, carry):
                z = i // slots_dev
                pair = (z // 2, z % 2)
                owner = bit * weight[dims[1]]
                for d, b in zip(others, pair):
                    owner += b * weight[d]
                which = r["inv"][owner * slots_dev + i % slots_dev]
                there = jnp.where(which >= 0, 1.0, 0.0)
                which = jnp.maximum(which, 0)
                value = r["ot"][which, at_rows, :] + r["rt"][which, at_rows, :].astype(f32)
                dst[pair + (i % slots_dev,)] = (value * there).astype(kind)
                return carry

            lax.fori_loop(0, slots_dev * n_tbl // 2, run, 0, unroll=5)

        bit = bits[dims[1]]
        each_slot(1 - bit, r["s%s1" % name], bf16)
        flying[name] = send(r["s%s1" % name], r["r%s1" % name], peers[dims[1]])
        each_slot(bit, r["o%s1" % name], f32)

    def finish(name):
        flying[name].wait()
        value = r["o%s3" % name][...] + r["r%s3" % name][...].astype(f32)
        if name in table:
            lo, hi, dims = table[name]
            table_ref[:, lo * rows : hi * rows, :] = value
        else:
            top, bottom, wide, dims = cross[name]
            value = value * scale
            for i, (kind, lo) in enumerate((top, bottom)):
                at = lo if kind == "u" else width + lo
                cross_ref[:, at : at + wide] = value[8 * i : 8 * i + 8]

    for step in order:
        kind, rest = step[0], step[1:]
        if kind == "T":
            table_group(int(rest))
        elif kind == "X":
            cross_piece(rest)
        elif rest == "4":
            finish(kind)
        elif rest == "1" and kind in table:
            spread(kind)
        else:
            halve(kind, (table if kind in table else cross)[kind][-1], int(rest) - 1)


def copy_body(cross_ref, table_ref, cross_out, table_out, sems):
    copies = [
        pltpu.make_async_copy(cross_ref, cross_out, sems.at[0]),
        pltpu.make_async_copy(table_ref, table_out, sems.at[1]),
    ]
    for copy in copies:
        copy.start()
    for copy in copies:
        copy.wait()


def on_device_fused(cross_input, upstream, v_weight, u_weight, bias, placement, owned_ids):
    n_grp = lax.axis_size("grp")
    n_tbl = lax.axis_size("tbl")
    samples, width = cross_input.shape
    rank = v_weight.shape[0]
    slots_dev, hot = owned_ids.shape[:2]
    scale = 1.0 / math.sqrt(samples * n_grp * n_tbl)
    part = ROWS // n_grp
    plan = plan_of(width)
    scratch = scratch_of(samples, width, rank, n_tbl, slots_dev, hot, part, plan)
    vmem = pl.BlockSpec(memory_space=pltpu.VMEM)
    smem = pl.BlockSpec(memory_space=pltpu.SMEM)
    hbm = pl.BlockSpec(memory_space=pl.ANY)
    shapes = (
        jax.ShapeDtypeStruct((rank // (n_grp * n_tbl), 2 * width), jnp.float32),
        jax.ShapeDtypeStruct((slots_dev, part, EMB), jnp.float32),
    )
    sums = pl.pallas_call(
        functools.partial(fused_body, n_grp, n_tbl, scale, plan, tuple(scratch)),
        out_shape=tuple(pltpu.VMEM(s.shape, s.dtype) for s in shapes),
        in_specs=[hbm] * 4 + [vmem, smem, hbm],
        out_specs=(vmem, vmem),
        scratch_shapes=list(scratch.values()),
        compiler_params=pltpu.CompilerParams(
            collective_id=0, has_side_effects=True, vmem_limit_bytes=60 * 1024 * 1024
        ),
        name="cross_backward",
    )(
        cross_input, upstream, v_weight, u_weight,
        bias.reshape(width // EMB, EMB), placement, owned_ids,
    )
    return pl.pallas_call(
        copy_body,
        out_shape=shapes,
        in_specs=[vmem, vmem],
        out_specs=(hbm, hbm),
        scratch_shapes=[pltpu.SemaphoreType.DMA((2,))],
        name="hand_over",
    )(*[pltpu.with_memory_space_constraint(s, pltpu.VMEM) for s in sums])


def solution(mesh):
    in_specs = (
        P(("grp", "tbl"), None),
        P(("grp", "tbl"), None),
        P(),
        P(),
        P(),
        P(),
        P("tbl", None, "grp"),
    )
    out_specs = (P(("grp", "tbl"), None), P("tbl", "grp", None))
    fused = halving_fits(mesh.shape["grp"], mesh.shape["tbl"])
    return jax.shard_map(
        on_device_fused if fused else on_device, mesh=mesh, in_specs=in_specs, out_specs=out_specs, check_vma=False
    )
```

```python
import functools
import math

import jax
import jax.numpy as jnp
from jax import lax
from jax.experimental import pallas as pl
from jax.experimental.pallas import tpu as pltpu
from jax.sharding import PartitionSpec as P

EMB = 128
TABLES = 26
ROWS = 256
MESH = pl.DeviceIdType.MESH


def outer_sum(left, right):
    return jnp.einsum("br,bd->rd", left, right, preferred_element_type=jnp.float32)


def on_device(cross_input, upstream, v_weight, u_weight, bias, placement, owned_ids):
    n_grp = lax.axis_size("grp")
    n_tbl = lax.axis_size("tbl")
    samples = cross_input.shape[0]
    slots_dev = owned_ids.shape[0]
    scale = 1.0 / math.sqrt(samples * n_grp * n_tbl)
    hidden = jnp.dot(cross_input, v_weight.T, preferred_element_type=jnp.float32).astype(
        jnp.bfloat16
    )
    mixed = jnp.dot(hidden, u_weight, preferred_element_type=jnp.float32) + bias
    up_float = upstream.astype(jnp.float32)
    product_grad = (up_float * cross_input.astype(jnp.float32)).astype(jnp.bfloat16)
    hidden_grad = jnp.dot(product_grad, u_weight.T, preferred_element_type=jnp.float32).astype(
        jnp.bfloat16
    )
    input_grad = up_float * (1.0 + mixed) + jnp.dot(
        hidden_grad, v_weight, preferred_element_type=jnp.float32
    )
    pooled = input_grad[:, EMB:].astype(jnp.bfloat16).reshape(samples, TABLES, EMB)
    same = placement[:, None] == placement[None, :]
    earlier = jnp.arange(TABLES)[None, :] < jnp.arange(TABLES)[:, None]
    slot = jnp.sum((same & earlier).astype(jnp.int32), axis=1)
    target = slot * n_tbl + placement
    select = (jnp.arange(slots_dev * n_tbl, dtype=jnp.int32)[:, None] == target[None, :]).astype(
        jnp.bfloat16
    )
    outgoing = jnp.einsum("st,bte->sbe", select, pooled, preferred_element_type=jnp.float32)
    outgoing = outgoing.astype(jnp.bfloat16).reshape(slots_dev, n_tbl, samples, EMB)
    arriving = lax.all_to_all(outgoing, "tbl", split_axis=1, concat_axis=1, tiled=True)
    arriving = arriving.reshape(slots_dev, n_tbl * samples, EMB)
    row_numbers = jnp.arange(ROWS, dtype=jnp.int32)
    counts = jnp.sum(
        (owned_ids[:, :, None, :] == row_numbers[None, None, :, None]).astype(jnp.bfloat16), axis=1
    )
    row_terms = jnp.einsum("srm,sme->sre", counts, arriving, preferred_element_type=jnp.float32)
    table_grad = lax.psum_scatter(row_terms, "grp", scatter_dimension=1, tiled=True)
    term = jnp.concatenate(
        [outer_sum(hidden, product_grad), outer_sum(hidden_grad, cross_input)], axis=1
    )
    summed = lax.psum_scatter(term, ("grp", "tbl"), scatter_dimension=0, tiled=True)
    cross_grad = summed * scale
    return (cross_grad, table_grad)


def halving_fits(n_grp, n_tbl):
    return n_grp == 4 and n_tbl == 8


CANON = "xhly"


def left_over(done):
    return [d for d in CANON if d not in done]


def lead_of(done):
    return (2,) * len(left_over(done))


def plan_of(width):
    tiles = width // EMB
    ends = [tiles * n // 27 * EMB for n in (0, 6, 9, 13, 16, 20, 24, 27)]
    dims = ("yxlh", "lhyx", "yxlh", "lhyx", "lhxy", "ylxh", "ylxh")
    cross = {}
    for i, name in enumerate("abcdefg"):
        cross[name] = (("u", ends[i]), ("v", ends[i]), ends[i + 1] - ends[i], dims[i])
    table = {}
    for i, rest in enumerate(("yhl", "ylh", "ylh", "lyh")):
        table["ABCD"[i]] = (i, i + 1, "x" + rest)
    groups = (0, 8, 16, 22, 26)
    order = (
        ["Xb", "Xg", "T0", "Xa", "Xd", "T1", "Xf", "Xe", "Xc", "T2", "T3", "b1", "g1", "d1", "a1", "e1", "b2", "g2", "f1", "A1", "B1", "C1", "D1", "d2", "c1", "a2", "b3", "g3", "f2", "e2", "A2", "c2", "D2", "b4", "B2", "e3", "a3", "f3", "g4", "C2", "d3", "c3", "A3", "D3", "B3", "e4", "d4", "a4", "f4", "C3", "A4", "c4", "B4", "D4", "C4"]
    )
    return cross, table, groups, order


def scratch_of(samples, width, rank, n_tbl, slots_dev, hot, part, plan):
    f32, bf16, i32 = jnp.float32, jnp.bfloat16, jnp.int32
    V = pltpu.VMEM
    cross, table, groups, order = plan
    rows = part // len(table)
    out = {
        "ci": V((2 * samples, width), bf16),
        "up": V((2 * samples, width), bf16),
        "v": V((rank, width), bf16),
        "u": V((rank, width), bf16),
        "pg": V((2 * samples, width), bf16),
        "hid": V((2 * samples, rank), bf16),
        "hgr": V((2 * samples, rank), bf16),
        "hid_t": V((2, rank, samples), bf16),
        "hgr_t": V((2, rank, samples), bf16),
        "ids": V((2, n_tbl, slots_dev, hot, samples), i32),
        "slot": pltpu.SMEM((TABLES,), i32),
        "inv": pltpu.SMEM((slots_dev * n_tbl,), i32),
        "load_sem": pltpu.SemaphoreType.DMA((4,)),
        "in_s": pltpu.SemaphoreType.DMA((10,)),
        "in_r": pltpu.SemaphoreType.DMA((10,)),
        "id_s": pltpu.SemaphoreType.DMA((2, n_tbl)),
        "id_r": pltpu.SemaphoreType.DMA((2, n_tbl)),
        "ssem": pltpu.SemaphoreType.DMA((64,)),
        "rsem": pltpu.SemaphoreType.DMA((64,)),
        "st": V((TABLES, part, EMB), bf16),
        "rt": V((TABLES, part, EMB), bf16),
        "ot": V((TABLES, part, EMB), f32),
    }
    for name, (top, bottom, wide, dims) in cross.items():
        for k in range(4):
            shape = lead_of(dims[: k + 1]) + (16, wide)
            out["s%s%d" % (name, k)] = V(shape, bf16)
            out["r%s%d" % (name, k)] = V(shape, bf16)
            out["o%s%d" % (name, k)] = V(shape, f32)
    for name, (lo, hi, dims) in table.items():
        for k in range(1, 4):
            shape = lead_of(dims[: k + 1]) + (slots_dev, rows, EMB)
            out["s%s%d" % (name, k)] = V(shape, bf16)
            out["r%s%d" % (name, k)] = V(shape, bf16)
            out["o%s%d" % (name, k)] = V(shape, f32)
    return out


def fused_body(n_grp, n_tbl, scale, plan, names, *refs):
    f32, bf16 = jnp.float32, jnp.bfloat16
    ci_hbm, up_hbm, v_hbm, u_hbm, bias_ref, place_ref, ids_hbm, cross_ref, table_ref = refs[:9]
    r = dict(zip(names, refs[9:]))
    cross, table, groups, order = plan
    g = lax.axis_index("grp")
    t = lax.axis_index("tbl")
    core, x = g % 2, g // 2
    y, zl, zh = t % 2, (t // 2) % 2, t // 4
    og = g + 1 - 2 * core
    bits = {"x": x, "h": zh, "l": zl, "y": y}
    peers = {
        "x": (core + 2 * (1 - x), t),
        "y": (g, t + 1 - 2 * y),
        "l": (g, t + 2 * (1 - 2 * zl)),
        "h": (g, t + 4 * (1 - 2 * zh)),
    }
    samples, width = ci_hbm.shape
    rank = v_hbm.shape[0]
    slots_dev = ids_hbm.shape[0]
    part = ROWS // n_grp
    rows = part // len(table)
    quarter = rank // n_grp

    barrier = pltpu.get_barrier_semaphore()

    def greet(gg, tt):
        pl.semaphore_signal(barrier, inc=1, device_id=(gg, tt), device_id_type=MESH)

    for step in range(1, n_tbl):
        greet(g, (t + step) % n_tbl)
        greet(og, (t + step) % n_tbl)
    greet(og, t)
    greet(*peers["x"])

    own_rows, their_rows = pl.ds(0, samples), pl.ds(samples, samples)
    loads = [
        pltpu.make_async_copy(src, dst, r["load_sem"].at[i])
        for i, (src, dst) in enumerate(
            (
                (ci_hbm, r["ci"].at[own_rows]),
                (v_hbm, r["v"]),
                (up_hbm, r["up"].at[own_rows]),
                (u_hbm, r["u"]),
            )
        )
    ]
    for load in loads:
        load.start()

    pl.semaphore_wait(barrier, 2 * n_tbl)

    def remote(src, dst, s, rs, peer):
        copy = pltpu.make_async_remote_copy(
            src_ref=src, dst_ref=dst, send_sem=s, recv_sem=rs,
            device_id=peer, device_id_type=MESH,
        )
        copy.start()
        return copy

    sems = iter(range(64))

    def send(src, dst, peer):
        i = next(sems)
        return remote(src, dst, r["ssem"].at[i], r["rsem"].at[i], peer)

    thirds = [width // EMB * i // 3 * EMB for i in range(4)]
    moves = []
    for i in range(3):
        cols = pl.ds(thirds[i], thirds[i + 1] - thirds[i])
        moves.append((ci_hbm.at[:, cols], r["ci"].at[their_rows, cols]))
        moves.append((up_hbm.at[:, cols], r["up"].at[their_rows, cols]))
    raw = [
        remote(src, dst, r["in_s"].at[i], r["in_r"].at[i], (og, t))
        for i, (src, dst) in enumerate(moves)
    ]
    id_copies = []
    for step in range(n_tbl):
        to = (t + step) % n_tbl
        block = ids_hbm.at[:, :, pl.ds(pl.multiple_of(to * samples, samples), samples)]
        if step == 0:
            mine = pltpu.make_async_copy(block, r["ids"].at[0, t], r["id_s"].at[0, 0])
            mine.start()
        else:
            id_copies.append(
                remote(
                    block, r["ids"].at[0, t], r["id_s"].at[0, step], r["id_r"].at[0, step], (g, to)
                )
            )
        id_copies.append(
            remote(block, r["ids"].at[1, t], r["id_s"].at[1, step], r["id_r"].at[1, step], (og, to))
        )

    nt = (((1,), (1,)), ((), ()))

    def by_position(value):
        blocks = []
        for gg in range(n_grp):
            for pos in range(n_tbl):
                yy, ll, hh = pos // 4, (pos // 2) % 2, pos % 2
                at = gg * quarter + 8 * (hh * 4 + ll * 2 + yy)
                blocks.append(value[at : at + 8])
        return jnp.concatenate(blocks, axis=0).astype(bf16)

    loads[0].wait()
    loads[1].wait()
    hidden = lax.dot_general(r["ci"][own_rows, :], r["v"][...], nt, preferred_element_type=f32)
    r["hid"][own_rows, :] = hidden.astype(bf16)
    r["hid_t"][0] = by_position(hidden.T)
    at = 6
    ready = []
    for i, (src, dst) in enumerate(
        (
            (r["hid_t"].at[0], r["hid_t"].at[1]),
            (r["hid"].at[own_rows], r["hid"].at[their_rows]),
        )
    ):
        ready.append(remote(src, dst, r["in_s"].at[at + i], r["in_r"].at[at + i], (og, t)))
    loads[2].wait()
    loads[3].wait()
    places = [place_ref[i] for i in range(TABLES)]
    targets = []
    for i in range(TABLES):
        slot = jnp.int32(0)
        for j in range(i):
            slot += (places[j] == places[i]).astype(jnp.int32)
        r["slot"][i] = jnp.minimum(slot, slots_dev - 1)
        targets.append(places[i] * slots_dev + slot)
    for q in range(slots_dev * n_tbl):
        which = jnp.int32(-1)
        for i in range(TABLES):
            which = jnp.where(targets[i] == q, i, which)
        r["inv"][q] = which
    r["pg"][own_rows, :] = (
        r["up"][own_rows, :].astype(f32) * r["ci"][own_rows, :].astype(f32)
    ).astype(bf16)
    hgrad = lax.dot_general(r["pg"][own_rows, :], r["u"][...], nt, preferred_element_type=f32)
    r["hgr"][own_rows, :] = hgrad.astype(bf16)
    r["hgr_t"][0] = by_position(hgrad.T)
    for i, (src, dst) in enumerate(
        (
            (r["hgr_t"].at[0], r["hgr_t"].at[1]),
            (r["hgr"].at[own_rows], r["hgr"].at[their_rows]),
        )
    ):
        ready.append(remote(src, dst, r["in_s"].at[at + 2 + i], r["in_r"].at[at + 2 + i], (og, t)))

    index = lax.broadcasted_iota(jnp.int32, (2 * part, 2 * samples), 0)
    side_of = jnp.where(index // part == 0, x, 1 - x)
    row_of = ((side_of * 2 + core) * part + index % part).astype(f32).astype(bf16)

    def tables(pair):
        cols = pl.ds(EMB + pair * 2 * EMB, 2 * EMB)
        shift = jnp.concatenate(
            [bias_ref[pl.ds(1 + 2 * pair, 1), :], bias_ref[pl.ds(2 + 2 * pair, 1), :]], axis=1
        )
        mixed = jnp.dot(r["hid"][...], r["u"][:, cols], preferred_element_type=f32) + shift
        back = jnp.dot(r["hgr"][...], r["v"][:, cols], preferred_element_type=f32)
        pooled = (r["up"][:, cols].astype(f32) * (1.0 + mixed) + back).astype(bf16)
        for piece in range(2):
            which = pair * 2 + piece
            owner, slot = place_ref[which], r["slot"][which]
            looked = jnp.concatenate([r["ids"][0, owner, slot], r["ids"][1, owner, slot]], axis=1)
            looked = looked.astype(f32).astype(bf16)
            one, zero = jnp.bfloat16(1), jnp.bfloat16(0)
            count = jnp.zeros((2 * part, 2 * samples), bf16)
            for k in range(looked.shape[0]):
                count += jnp.where(looked[k : k + 1, :] == row_of, one, zero)
            sums = jnp.dot(
                count, pooled[:, piece * EMB : (piece + 1) * EMB], preferred_element_type=f32
            )
            r["ot"][which] = sums[:part]
            r["st"][which] = sums[part:].astype(bf16)

    def picked(ref, first):
        def take(gg, start, size):
            at = pl.ds(pl.multiple_of(gg * quarter + start, size), size)
            return jnp.concatenate([ref[0, at, :], ref[1, at, :]], axis=1)

        out = []
        for side in range(2):
            bit = bits[first] if side == 0 else 1 - bits[first]
            if first == "x":
                out.append(take(core + 2 * bit, 0, quarter))
                continue
            for xx in range(2):
                if first == "y":
                    out.append(take(core + 2 * xx, bit * (quarter // 2), quarter // 2))
                else:
                    for yy in range(2):
                        out.append(
                            take(
                                core + 2 * xx, yy * (quarter // 2) + bit * (quarter // 4), quarter // 4
                            )
                        )
        return jnp.concatenate(out, axis=0)

    def place_of(first, i):
        a, b, c = i // 4, (i // 2) % 2, i % 2
        if first == "y":
            return (a, c, b)
        if first == "l":
            return (a, c, b)
        return (c, b, a)

    flying, chosen, waited = {}, {}, set()

    def await_all(key, copies):
        if key not in waited:
            waited.add(key)
            for copy in copies:
                copy.wait()

    def raw_ready(lo, hi):
        for i in range(3):
            if lo < thirds[i + 1] and hi > thirds[i]:
                await_all("raw%d" % i, raw[2 * i : 2 * i + 2])

    made_pg = set()

    def factors(kind, first):
        index = 0 if kind == "u" else 2
        await_all("ready%d" % index, [ready[index]])
        if (kind, first) not in chosen:
            chosen[kind, first] = picked(r["hid_t" if kind == "u" else "hgr_t"], first)
        return chosen[kind, first]

    def product(kind, lhs, lo, hi):
        if kind == "v":
            return jnp.dot(lhs, r["ci"][:, lo:hi], preferred_element_type=f32)
        theirs = (
            r["up"][their_rows, lo:hi].astype(f32) * r["ci"][their_rows, lo:hi].astype(f32)
        ).astype(bf16)
        both = jnp.concatenate([r["pg"][own_rows, lo:hi], theirs], axis=0)
        return jnp.dot(lhs, both, preferred_element_type=f32)

    def cross_piece(name):
        top, bottom, wide, dims = cross[name]
        for kind, lo in (top, bottom):
            raw_ready(lo, lo + wide)
        for off in range(0, wide, 512):
            end = min(off + 512, wide)
            halves = []
            for kind, lo in (top, bottom):
                halves.append(product(kind, factors(kind, dims[0]), lo + off, lo + end))
            for i in range(2 * n_tbl):
                tile = jnp.concatenate([h[8 * i : 8 * i + 8] for h in halves], axis=0)
                at = place_of(dims[0], i % n_tbl) + (slice(None), slice(off, end))
                if i < n_tbl:
                    r["o%s0" % name][at] = tile
                else:
                    r["s%s0" % name][at] = tile.astype(bf16)
        flying[name] = send(r["s%s0" % name], r["r%s0" % name], peers[dims[0]])

    def table_group(n):
        await_all("ready1", [ready[1]])
        await_all("ready3", [ready[3]])
        raw_ready(EMB * (1 + groups[n]), EMB * (1 + groups[n + 1]))
        await_all("ids", [mine] + id_copies)
        for pair in range(groups[n] // 2, groups[n + 1] // 2):
            tables(pair)
        at = pl.ds(groups[n], groups[n + 1] - groups[n])
        flying["T%d" % n] = send(r["st"].at[at], r["rt"].at[at], peers["x"])

    def indices(depth):
        out = [()]
        for _ in range(depth):
            out = [i + (j,) for i in out for j in range(2)]
        return out

    def halve(name, dims, k):
        flying[name].wait()
        own, came = r["o%s%d" % (name, k)], r["r%s%d" % (name, k)]
        kept, out = r["o%s%d" % (name, k + 1)], r["s%s%d" % (name, k + 1)]
        axis = left_over(dims[: k + 1]).index(dims[k + 1])
        bit = bits[dims[k + 1]]

        def fill(dst, b, kind):
            for i in indices(2 - k):
                at = i[:axis] + (b,) + i[axis:]
                value = (own[at] + came[at].astype(f32)).astype(kind)
                if i:
                    dst[i] = value
                else:
                    dst[...] = value

        fill(out, 1 - bit, bf16)
        flying[name] = send(out, r["r%s%d" % (name, k + 1)], peers[dims[k + 1]])
        fill(kept, bit, f32)

    def spread(name):
        lo, hi, dims = table[name]
        for n in range(len(groups) - 1):
            await_all("T%d" % n, [flying["T%d" % n]])
        others = left_over(dims[:2])
        weight = {"h": 4, "l": 2, "y": 1}
        at_rows = pl.ds(lo * rows, (hi - lo) * rows)

        def each_slot(bit, dst, kind):
            def run(i, carry):
                z = i // slots_dev
                pair = (z // 2, z % 2)
                owner = bit * weight[dims[1]]
                for d, b in zip(others, pair):
                    owner += b * weight[d]
                which = r["inv"][owner * slots_dev + i % slots_dev]
                there = jnp.where(which >= 0, 1.0, 0.0)
                which = jnp.maximum(which, 0)
                value = r["ot"][which, at_rows, :] + r["rt"][which, at_rows, :].astype(f32)
                dst[pair + (i % slots_dev,)] = (value * there).astype(kind)
                return carry

            lax.fori_loop(0, slots_dev * n_tbl // 2, run, 0, unroll=True)

        bit = bits[dims[1]]
        each_slot(1 - bit, r["s%s1" % name], bf16)
        flying[name] = send(r["s%s1" % name], r["r%s1" % name], peers[dims[1]])
        each_slot(bit, r["o%s1" % name], f32)

    def finish(name):
        flying[name].wait()
        value = r["o%s3" % name][...] + r["r%s3" % name][...].astype(f32)
        if name in table:
            lo, hi, dims = table[name]
            table_ref[:, lo * rows : hi * rows, :] = value
        else:
            top, bottom, wide, dims = cross[name]
            value = value * scale
            for i, (kind, lo) in enumerate((top, bottom)):
                at = lo if kind == "u" else width + lo
                cross_ref[:, at : at + wide] = value[8 * i : 8 * i + 8]

    for step in order:
        kind, rest = step[0], step[1:]
        if kind == "T":
            table_group(int(rest))
        elif kind == "X":
            cross_piece(rest)
        elif rest == "4":
            finish(kind)
        elif rest == "1" and kind in table:
            spread(kind)
        else:
            halve(kind, (table if kind in table else cross)[kind][-1], int(rest) - 1)


def copy_body(cross_ref, table_ref, cross_out, table_out, sems):
    copies = [
        pltpu.make_async_copy(cross_ref, cross_out, sems.at[0]),
        pltpu.make_async_copy(table_ref, table_out, sems.at[1]),
    ]
    for copy in copies:
        copy.start()
    for copy in copies:
        copy.wait()


def on_device_fused(cross_input, upstream, v_weight, u_weight, bias, placement, owned_ids):
    n_grp = lax.axis_size("grp")
    n_tbl = lax.axis_size("tbl")
    samples, width = cross_input.shape
    rank = v_weight.shape[0]
    slots_dev, hot = owned_ids.shape[:2]
    scale = 1.0 / math.sqrt(samples * n_grp * n_tbl)
    part = ROWS // n_grp
    plan = plan_of(width)
    scratch = scratch_of(samples, width, rank, n_tbl, slots_dev, hot, part, plan)
    vmem = pl.BlockSpec(memory_space=pltpu.VMEM)
    smem = pl.BlockSpec(memory_space=pltpu.SMEM)
    hbm = pl.BlockSpec(memory_space=pl.ANY)
    shapes = (
        jax.ShapeDtypeStruct((rank // (n_grp * n_tbl), 2 * width), jnp.float32),
        jax.ShapeDtypeStruct((slots_dev, part, EMB), jnp.float32),
    )
    sums = pl.pallas_call(
        functools.partial(fused_body, n_grp, n_tbl, scale, plan, tuple(scratch)),
        out_shape=tuple(pltpu.VMEM(s.shape, s.dtype) for s in shapes),
        in_specs=[hbm] * 4 + [vmem, smem, hbm],
        out_specs=(vmem, vmem),
        scratch_shapes=list(scratch.values()),
        compiler_params=pltpu.CompilerParams(
            collective_id=0, has_side_effects=True, vmem_limit_bytes=60 * 1024 * 1024
        ),
        name="cross_backward",
    )(
        cross_input, upstream, v_weight, u_weight,
        bias.reshape(width // EMB, EMB), placement, owned_ids,
    )
    return pl.pallas_call(
        copy_body,
        out_shape=shapes,
        in_specs=[vmem, vmem],
        out_specs=(hbm, hbm),
        scratch_shapes=[pltpu.SemaphoreType.DMA((2,))],
        name="hand_over",
    )(*[pltpu.with_memory_space_constraint(s, pltpu.VMEM) for s in sums])


def solution(mesh):
    in_specs = (
        P(("grp", "tbl"), None),
        P(("grp", "tbl"), None),
        P(),
        P(),
        P(),
        P(),
        P("tbl", None, "grp"),
    )
    out_specs = (P(("grp", "tbl"), None), P("tbl", "grp", None))
    fused = halving_fits(mesh.shape["grp"], mesh.shape["tbl"])
    return jax.shard_map(
        on_device_fused if fused else on_device, mesh=mesh, in_specs=in_specs, out_specs=out_specs, check_vma=False
    )
```
